32 devices in a mesh: dp: 8 (over y, x, core), tensor: 4 (over z).
Axes of the slice: x: 2, y: 2, z: 4, core: 2. Of those that a mesh axis runs over, the one named last changes fastest.
Arguments:
- tokens: bfloat16 [16384, 1024], P(('dp', 'tensor')), may hold values from -6 to 6
- lengths: int32 [8, 8], P('dp'), may hold values from 1 to 1024, 2048 in all within a row
- order: int32 [8, 2048], P('dp'), may hold values from 0 to 2047, each once within a row
- gain_attn: bfloat16 [1024], P('dp'), may hold values from 0.5 to 1.5
- w_qkv: bfloat16 [1024, 3, 1024], P('dp', None, 'tensor'), may hold values from -0.1875 to 0.1875
- w_attn_out: bfloat16 [1024, 1024], P('tensor', 'dp'), may hold values from -0.75 to 0.75
- gain_mlp: bfloat16 [1024], P('dp'), may hold values from 0.5 to 1.5
- w_in: bfloat16 [1024, 2, 2624], P('dp', None, 'tensor'), may hold values from -0.1875 to 0.1875
- w_mlp_out: bfloat16 [2624, 1024], P('tensor', 'dp'), may hold values from -0.125 to 0.125
- grad_out: bfloat16 [16384, 1024], P(('dp', 'tensor')), may hold values from -6 to 6
Outputs:
- result: bfloat16 [16384, 1024], P(('dp', 'tensor'))
- grad_tokens: bfloat16 [16384, 1024], P(('dp', 'tensor'))
- grad_gain_attn: float32 [1024], P('dp')
- grad_qkv: float32 [1024, 3, 1024], P('dp', None, 'tensor')
- grad_attn_out: float32 [1024, 1024], P('tensor', 'dp')
- grad_gain_mlp: float32 [1024], P('dp')
- grad_in: float32 [1024, 2, 2624], P('dp', None, 'tensor')
- grad_mlp_out: float32 [2624, 1024], P('tensor', 'dp')
The draws below stay inside these ranges and needn't reach their ends.
Inputs may be any that keep to these rules, and one draw needn't show every extreme that they name: Each row of lengths sums to 2048; every group's longest sequence has exactly 1024 rows. Each row of order holds every number below 2048 once.
All inputs are finite; a program needn't handle non-finite values.
Results may differ from the reference program's by a relative error of at most 0.017.
Values may be sent and summed in bfloat16 or wider, within the bound.
No kernel may reach another device: no remote copies, remote signals or barrier semaphores. Data moves between devices by JAX's collectives and lax.ppermute only.
A program may use at most 192 MiB of HBM per device.

```python
import math
import jax
import jax.numpy as jnp
import numpy as np
from jax import lax

D = 1024
HEADS = 16
HD = 64
FF = 2624
SLOTS = 8
GROUP_TOK = 2048
MAXLEN = 1024
TOKENS = 16384
N_DP = 8


def levels(stream_key, shape, split, least, top_value):
    def one(dim, blocks):
        draws = jax.random.uniform(jax.random.fold_in(jax.random.fold_in(stream_key, 6), dim), (blocks,), jnp.float32, least / len(split), top_value / len(split))
        return jnp.repeat(jnp.exp(draws), shape[dim] // blocks).reshape((-1,) + (1,) * (len(shape) - dim - 1))

    gain = one(*split[0])
    for cut in split[1:]:
        gain = gain * one(*cut)
    return gain


def profile(number_of, total, reach, slope):
    loads = [(1 << 20) // math.isqrt(grade ** slope) + 1 for grade in range(2, number_of + 1)]
    spare, given = total - reach - (number_of - 1), [1] * (number_of - 1)
    while spare > 0:
        candidates = [i for i in range(number_of - 1) if given[i] < reach]
        mass, budget = sum([loads[i] for i in candidates]), spare
        for i in candidates:
            more = min(reach - given[i], max(1, budget * loads[i] // mass), spare)
            given[i] = given[i] + more
            spare = spare - more
    return np.array([reach] + given)


def ragged_sizes(rng, number_of, total, limit, slope):
    if number_of == 2:
        one = jax.random.randint(rng, (), max(1, total - limit), min(limit, total - 1) + 1)
        return jnp.stack([one, total - one])
    sizes = jnp.asarray(profile(number_of, total, limit, slope), jnp.int32)
    twos = (number_of - 1) // 2
    donor, taker = sizes[1:1 + 2 * twos:2], sizes[2:2 + 2 * twos:2]
    slack = jnp.minimum(donor - 1, limit - taker)
    shifted = jax.random.randint(jax.random.fold_in(rng, 1), (twos,), 0, 1 << 20) % (slack + 1)
    sizes = sizes.at[1:1 + 2 * twos:2].set(donor - shifted).at[2:2 + 2 * twos:2].set(taker + shifted)
    return sizes[jax.random.permutation(jax.random.fold_in(rng, 2), number_of)]


def normal_values(own_key, extent, scale, most, split=(), held_as=jnp.bfloat16):
    result = scale * jax.random.normal(own_key, extent, jnp.float32)
    if split:
        result = result * levels(own_key, extent, split, -0.22, 0.18)
    return jnp.clip(result, -most, most).astype(held_as)


def setup_inputs(seed: int = 0) -> dict:
    key_list = jax.random.split(jax.random.key(seed), 11)
    tokens = normal_values(key_list[0], (TOKENS, D), 1.0, 6.0, ((0, 32),))
    lengths = jax.vmap(lambda own: ragged_sizes(own, SLOTS, GROUP_TOK, MAXLEN, 2))(jax.random.split(key_list[1], N_DP)).reshape((N_DP, SLOTS)).astype(jnp.int32)
    order = jax.vmap(lambda own: jax.random.permutation(own, GROUP_TOK))(jax.random.split(key_list[2], N_DP)).reshape((N_DP, GROUP_TOK)).astype(jnp.int32)
    gain_attn = jnp.clip(1.0 + 0.1 * jax.random.normal(key_list[3], (D,), jnp.float32), 0.5, 1.5).astype(jnp.bfloat16)
    w_qkv = normal_values(key_list[4], (D, 3, D), D ** -0.5, 0.1875, ((0, 8), (2, 4)))
    w_attn_out = normal_values(key_list[5], (D, D), (D // 16) ** -0.5, 0.75, ((0, 4), (1, 8)))
    gain_mlp = jnp.clip(1.0 + 0.1 * jax.random.normal(key_list[6], (D,), jnp.float32), 0.5, 1.5).astype(jnp.bfloat16)
    w_in = normal_values(key_list[7], (D, 2, FF), D ** -0.5, 0.1875, ((0, 8), (2, 4)))
    w_mlp_out = normal_values(key_list[8], (FF, D), FF ** -0.5, 0.125, ((0, 4), (1, 8)))
    grad_out = normal_values(key_list[9], (TOKENS, D), 1.0, 6.0, ((0, 32),))
    return dict(tokens=tokens, lengths=lengths, order=order, gain_attn=gain_attn, w_qkv=w_qkv, w_attn_out=w_attn_out, gain_mlp=gain_mlp, w_in=w_in, w_mlp_out=w_mlp_out, grad_out=grad_out)


EPS = 1e-05
THETA = 160000.0
NEG = -1e+30
HIGH = lax.Precision.HIGHEST

@jax.custom_vjp
def low(v):
    return lax.optimization_barrier(v.astype(jnp.bfloat16)).astype(jnp.float32)

@jax.custom_vjp
def low_back(v):
    return v

def low_keep(v):
    return (low(v), None)

def low_pass(kept, grad):
    return (grad,)

def back_keep(v):
    return (v, None)

def back_low(kept, grad):
    return (low(grad),)
low.defvjp(low_keep, low_pass)
low_back.defvjp(back_keep, back_low)

def norm_rows(values, gain_row):
    average = lax.optimization_barrier(jnp.mean(values, axis=-1, keepdims=True))
    centred = values - average
    spread = lax.optimization_barrier(jnp.mean(centred * centred, axis=-1, keepdims=True))
    return centred * lax.rsqrt(spread + EPS) * gain_row

def places(order_row, length_row):
    bounds = jnp.cumsum(length_row)
    passed = (order_row[:, None] >= bounds[None, :]).astype(jnp.int32)
    segment = lax.optimization_barrier(jnp.sum(passed, axis=1))
    offset = order_row - lax.optimization_barrier(jnp.sum(passed * length_row[None, :], axis=1))
    return (segment, offset)

def rotate(values, offset, turned):
    middle = values.shape[-1] // 2
    inverse = THETA ** (-2.0 * jnp.arange(middle, dtype=jnp.float32) / values.shape[-1])
    angles = offset.astype(jnp.float32)[:, None] * inverse[None, :]
    cosine = jnp.cos(angles)[:, None, :]
    sine_values = turned * jnp.sin(angles)[:, None, :]
    leading = values[..., :middle]
    trailing = values[..., middle:]
    return jnp.concatenate([leading * cosine - trailing * sine_values, trailing * cosine + leading * sine_values], axis=-1)

def group_layer(rows_in, segment, offset, gain_one, qkv_full, attn_out_full, gain_two, in_full, mlp_out_full):
    count_rows = rows_in.shape[0]
    normed_one = low(norm_rows(rows_in, gain_one))
    projected = low_back(jnp.einsum('rd,dce->rce', normed_one, qkv_full, precision=HIGH))
    queries = low(rotate(projected[:, 0].reshape(count_rows, HEADS, HD), offset, 1.0))
    keys_rot = low(rotate(projected[:, 1].reshape(count_rows, HEADS, HD), offset, 1.0))
    values_in = low(projected[:, 2].reshape(count_rows, HEADS, HD))
    scores = low_back(jnp.einsum('qhe,khe->hqk', queries, keys_rot, precision=HIGH) * HD ** (-0.5))
    same = (segment[:, None] == segment[None, :])[None]
    scores = jnp.where(same, scores, NEG)
    probs_low = low(jax.nn.softmax(scores, axis=-1))
    attended = jnp.einsum('hqk,khe->qhe', probs_low, values_in, precision=HIGH).reshape(count_rows, D)
    attended = low(low_back(attended))
    middle = rows_in + low_back(jnp.dot(attended, attn_out_full, precision=HIGH))
    normed_two = low(norm_rows(middle, gain_two))
    gate_up = low_back(jnp.einsum('rd,dcf->rcf', normed_two, in_full, precision=HIGH))
    activated = low(jax.nn.gelu(gate_up[:, 0], approximate=False) * gate_up[:, 1])
    return middle + low_back(jnp.dot(activated, mlp_out_full, precision=HIGH))

def reference(tokens, lengths, order, gain_attn, w_qkv, w_attn_out, gain_mlp, w_in, w_mlp_out, grad_out):
    groups = lengths.shape[0]
    segment, offset = jax.vmap(places)(order, lengths)
    inputs = tokens.astype(jnp.float32).reshape(groups, -1, D)
    cotangent = grad_out.astype(jnp.float32).reshape(groups, -1, D)

    def forward(rows_all, gain_one, qkv_full, attn_out_full, gain_two, in_full, mlp_out_full):

        def one_group(item):
            rows_in, segment_row, offset_row = item
            return group_layer(rows_in, segment_row, offset_row, gain_one, qkv_full, attn_out_full, gain_two, in_full, mlp_out_full)
        return lax.map(jax.checkpoint(one_group), (rows_all, segment, offset))
    outputs, pull = jax.vjp(forward, inputs, gain_attn.astype(jnp.float32), w_qkv.astype(jnp.float32), w_attn_out.astype(jnp.float32), gain_mlp.astype(jnp.float32), w_in.astype(jnp.float32), w_mlp_out.astype(jnp.float32))
    grads = pull(cotangent)
    return (outputs.reshape(TOKENS, D).astype(jnp.bfloat16), grads[0].reshape(TOKENS, D).astype(jnp.bfloat16), grads[1], grads[2], grads[3], grads[4], grads[5], grads[6])
```

```python
import jax
import jax.numpy as jnp
from jax import lax
from jax.sharding import PartitionSpec as P

HD = 64
EPS = 1e-05
THETA = 160000.0
NEG = -1e30
F32 = jnp.float32
BF16 = jnp.bfloat16


def dot(a, b, da, db):
    return lax.dot_general(a, b, (((da,), (db,)), ((), ())), preferred_element_type=F32)


def gather_line(x, axis):
    n = lax.axis_size(axis)
    here = lax.axis_index(axis)
    to_low = [(i, i - 1) for i in range(1, n)]
    to_high = [(i, i + 1) for i in range(n - 1)]
    from_high, from_low = [x], [x]
    for _ in range(1, n):
        from_high.append(lax.ppermute(from_high[-1], axis, to_low))
        from_low.append(lax.ppermute(from_low[-1], axis, to_high))
    out = jnp.zeros((n,) + x.shape, x.dtype)
    out = lax.dynamic_update_index_in_dim(out, x, here, 0)
    for s in range(1, n):
        piece = jnp.where(here + s < n, from_high[s], from_low[n - s])
        out = lax.dynamic_update_index_in_dim(out, piece, (here + s) % n, 0)
    return out


def scatter_line(parts, axis):
    n = lax.axis_size(axis)
    here = lax.axis_index(axis)

    def take(j):
        return lax.dynamic_index_in_dim(parts, jnp.clip(j, 0, n - 1), 0, keepdims=False)

    low = high = None
    for s in range(1, n):
        send_low = take(here + s - n)
        send_high = take(here + n - s)
        if s > 1:
            send_low = (send_low.astype(F32) + low.astype(F32)).astype(BF16)
            send_high = (send_high.astype(F32) + high.astype(F32)).astype(BF16)
        low = lax.ppermute(send_low, axis, [(i, i - 1) for i in range(n - s, n)])
        high = lax.ppermute(send_high, axis, [(i, i + 1) for i in range(s)])
    return take(here).astype(F32) + low.astype(F32) + high.astype(F32)


def places(order_row, length_row):
    bounds = jnp.cumsum(length_row)
    passed = (order_row[:, None] >= bounds[None, :]).astype(jnp.int32)
    segment = jnp.sum(passed, axis=1)
    offset = order_row - jnp.sum(passed * length_row[None, :], axis=1)
    return (segment, offset)


def rotate(values, offset, turned):
    middle = values.shape[-1] // 2
    inverse = THETA ** (-2.0 * jnp.arange(middle, dtype=F32) / values.shape[-1])
    angles = offset.astype(F32)[:, None] * inverse[None, :]
    cosine = jnp.cos(angles)[:, None, :]
    sine_values = turned * jnp.sin(angles)[:, None, :]
    leading = values[..., :middle]
    trailing = values[..., middle:]
    return jnp.concatenate(
        [leading * cosine - trailing * sine_values, trailing * cosine + leading * sine_values],
        axis=-1,
    )


def block_scores(query_part, keys_rot, segment_part, segment, scale):
    scores = jnp.einsum("qhe,khe->hqk", query_part, keys_rot, preferred_element_type=F32) * scale
    return jnp.where((segment_part[:, None] == segment[None, :])[None], scores, NEG)


def attend(queries, keys_rot, values_in, segment):
    total_rows = queries.shape[0]
    block = min(512, total_rows)
    blocks = total_rows // block
    scale = queries.shape[-1] ** (-0.5)
    query_blocks = queries.reshape(blocks, block, queries.shape[1], queries.shape[2])
    segment_blocks = segment.reshape(blocks, block)

    def one_block(item):
        query_part, segment_part = item
        scores = block_scores(query_part, keys_rot, segment_part, segment, scale)
        highest = jnp.max(scores, axis=-1, keepdims=True)
        weights = jnp.exp(scores - highest)
        totals = jnp.sum(weights, axis=-1, keepdims=True)
        probs_low = (weights / totals).astype(BF16)
        mixed = jnp.einsum("hqk,khe->qhe", probs_low, values_in, preferred_element_type=F32)
        return (mixed.astype(BF16), highest[..., 0] + jnp.log(totals[..., 0]))

    mixed, logsum = lax.map(one_block, (query_blocks, segment_blocks))
    return (mixed.reshape(total_rows, -1), logsum)


def attend_back(queries, keys_rot, values_in, segment, logsum, grad_attended):
    total_rows = queries.shape[0]
    block = min(512, total_rows)
    blocks = total_rows // block
    scale = queries.shape[-1] ** (-0.5)
    query_blocks = queries.reshape(blocks, block, queries.shape[1], queries.shape[2])
    grad_blocks = grad_attended.reshape(blocks, block, queries.shape[1], queries.shape[2])
    segment_blocks = segment.reshape(blocks, block)

    def one_block(carry, item):
        grad_keys, grad_values = carry
        query_part, segment_part, logsum_part, grad_part = item
        scores = block_scores(query_part, keys_rot, segment_part, segment, scale)
        probabilities = jnp.exp(scores - logsum_part[..., None])
        probs_low = probabilities.astype(BF16)
        grad_values = grad_values + jnp.einsum(
            "hqk,qhe->khe", probs_low, grad_part, preferred_element_type=F32
        )
        grad_probs = jnp.einsum("qhe,khe->hqk", grad_part, values_in, preferred_element_type=F32)
        inner = jnp.sum(probabilities * grad_probs, axis=-1, keepdims=True)
        grad_scores = (probabilities * (grad_probs - inner)).astype(BF16)
        grad_query = (
            jnp.einsum("hqk,khe->qhe", grad_scores, keys_rot, preferred_element_type=F32) * scale
        )
        grad_keys = (
            grad_keys
            + jnp.einsum("hqk,qhe->khe", grad_scores, query_part, preferred_element_type=F32)
            * scale
        )
        return ((grad_keys, grad_values), grad_query)

    empty = jnp.zeros(keys_rot.shape, F32)
    (grad_keys, grad_values), grad_queries = lax.scan(
        one_block, (empty, empty), (query_blocks, segment_blocks, logsum, grad_blocks)
    )
    return (grad_queries.reshape(keys_rot.shape), grad_keys, grad_values)


def norm_parts(values):
    average = jnp.mean(values, axis=-1, keepdims=True)
    centred = values - average
    spread = jnp.mean(centred * centred, axis=-1, keepdims=True)
    scale = lax.rsqrt(spread + EPS)
    return centred * scale, scale


def norm_back(grad_n, xhat, scale, gain_row):
    e = grad_n * gain_row
    return (
        e
        - jnp.mean(e, axis=-1, keepdims=True)
        - xhat * jnp.mean(e * xhat, axis=-1, keepdims=True)
    ) * scale


def on_device(
    tokens, lengths, order, gain_attn, w_qkv, w_attn_out, gain_mlp, w_in, w_mlp_out, grad_out
):
    tensor_size = lax.axis_size("tensor")
    local_rows, width = tokens.shape
    group_rows = local_rows * tensor_size
    piece = w_qkv.shape[0]
    heads_wide = w_qkv.shape[2]
    heads_here = heads_wide // HD
    units = w_in.shape[2]
    all_units = units * tensor_size
    segment, offset = places(order[0], lengths[0])

    gains_low = jnp.zeros((16, piece), BF16).at[0].set(gain_attn).at[1].set(gain_mlp)
    qkv_rows = jnp.concatenate(
        [w_qkv.transpose(1, 2, 0).reshape(3 * heads_wide, piece), gains_low], axis=0
    )
    qkv_rows = lax.all_gather(qkv_rows, "dp", axis=1, tiled=True)
    qkv_t = qkv_rows[: 3 * heads_wide]
    gain_one = qkv_rows[3 * heads_wide].astype(F32)
    gain_two = qkv_rows[3 * heads_wide + 1].astype(F32)

    w_in_t = w_in.transpose(1, 2, 0)
    mine = jnp.concatenate([w_attn_out, w_in_t[0], w_in_t[1], w_mlp_out], axis=0)
    near = gather_line(mine, "tensor")
    rows_all = gather_line(tokens, "tensor").reshape(group_rows, width)
    cuts = [heads_wide, heads_wide + units, heads_wide + 2 * units]

    def over_dp(part):
        return lax.all_gather(part.reshape(-1, piece), "dp", axis=1, tiled=True)

    w_ao = over_dp(near[:, : cuts[0]])
    w_gate = over_dp(near[:, cuts[0] : cuts[1]])
    w_up = over_dp(near[:, cuts[1] : cuts[2]])
    w_down = over_dp(near[:, cuts[2] :])

    xhat_all, scale_all = norm_parts(rows_all.astype(F32))
    rows_one = (xhat_all * gain_one).astype(BF16)
    projected = dot(rows_one, qkv_t, 1, 1).reshape(group_rows, 3, heads_here, HD)
    queries = rotate(projected[:, 0], offset, 1.0).astype(BF16)
    keys_rot = rotate(projected[:, 1], offset, 1.0).astype(BF16)
    values_in = projected[:, 2].astype(BF16)
    mixed, logsum = attend(queries, keys_rot, values_in, segment)
    attended = lax.all_to_all(mixed, "tensor", split_axis=0, concat_axis=1, tiled=True)

    inputs = tokens.astype(F32)
    middle = inputs + dot(attended, w_ao, 1, 0)
    xhat_two, scale_two = norm_parts(middle)
    rows_two = (xhat_two * gain_two).astype(BF16)
    gate = dot(rows_two, w_gate, 1, 1)
    up = dot(rows_two, w_up, 1, 1)
    grad_act = dot(grad_out, w_down, 1, 1)
    cdf = 0.5 * (1.0 + lax.erf(gate * (0.5**0.5)))
    density = jnp.exp(-0.5 * gate * gate) * 0.3989422804014327
    bent = gate * cdf
    activated = (bent * up).astype(BF16)
    grad_gate = (grad_act * up * (cdf + gate * density)).astype(BF16)
    grad_up = (grad_act * bent).astype(BF16)
    result = (middle + dot(activated, w_down, 1, 0)).astype(BF16)
    grad_normed_two = dot(grad_gate, w_gate, 1, 0) + dot(grad_up, w_up, 1, 0)
    grad_middle = grad_out.astype(F32) + norm_back(grad_normed_two, xhat_two, scale_two, gain_two)
    gain_two_part = jnp.sum(grad_normed_two * xhat_two, axis=0)
    grad_branch = grad_middle.astype(BF16)
    grad_attended = dot(grad_branch, w_ao, 1, 1).astype(BF16)
    grad_attended = lax.all_to_all(
        grad_attended, "tensor", split_axis=1, concat_axis=0, tiled=True
    )

    def over_rows(a, b):
        return lax.psum_scatter(
            dot(a, b, 0, 0).astype(BF16), "dp", scatter_dimension=1, tiled=True
        )

    sum_down = over_rows(activated, grad_out)
    sum_gate = over_rows(grad_gate, rows_two)
    sum_up = over_rows(grad_up, rows_two)
    sum_ao = over_rows(attended, grad_branch)

    grad_queries, grad_keys, grad_values = attend_back(
        queries,
        keys_rot,
        values_in,
        segment,
        logsum,
        grad_attended.reshape(group_rows, heads_here, HD),
    )
    grad_projected = (
        jnp.stack(
            [rotate(grad_queries, offset, -1.0), rotate(grad_keys, offset, -1.0), grad_values],
            axis=1,
        )
        .astype(BF16)
        .reshape(group_rows, -1)
    )
    part_one = dot(grad_projected, qkv_t, 1, 0)
    gain_one_part = jnp.sum(part_one * xhat_all, axis=0)
    part_one = part_one.astype(BF16).reshape(tensor_size, local_rows, width)
    grad_normed_one = scatter_line(part_one, "tensor")
    grad_qkv_rows = dot(grad_projected, rows_one, 0, 0).astype(BF16)
    gain_rows = (
        jnp.zeros((16, width), F32).at[0].set(gain_one_part).at[1].set(gain_two_part).astype(BF16)
    )
    sum_qkv = lax.psum_scatter(
        jnp.concatenate([grad_qkv_rows, gain_rows], axis=0), "dp", scatter_dimension=1, tiled=True
    )
    gain_sums = lax.psum(sum_qkv[3 * heads_wide : 3 * heads_wide + 2].astype(F32), "tensor")

    xhat_one, scale_one = norm_parts(inputs)
    grad_tokens = grad_middle + norm_back(grad_normed_one, xhat_one, scale_one, gain_one)

    grads = jnp.concatenate(
        [
            s.reshape(tensor_size, -1, piece)
            for s in (sum_ao, sum_gate, sum_up, sum_down)
        ],
        axis=1,
    )
    grads = scatter_line(grads, "tensor")
    grad_ao = grads[: cuts[0]]
    grad_in = jnp.stack([grads[cuts[0] : cuts[1]], grads[cuts[1] : cuts[2]]]).transpose(2, 0, 1)
    grad_down = grads[cuts[2] :]
    grad_qkv = (
        sum_qkv[: 3 * heads_wide].astype(F32).reshape(3, heads_wide, piece).transpose(2, 0, 1)
    )
    return (
        result,
        grad_tokens.astype(BF16),
        gain_sums[0],
        grad_qkv,
        grad_ao,
        gain_sums[1],
        grad_in,
        grad_down,
    )


def solution(mesh):
    in_specs = (
        P(("dp", "tensor"), None),
        P("dp", None),
        P("dp", None),
        P("dp"),
        P("dp", None, "tensor"),
        P("tensor", "dp"),
        P("dp"),
        P("dp", None, "tensor"),
        P("tensor", "dp"),
        P(("dp", "tensor"), None),
    )
    out_specs = (
        P(("dp", "tensor"), None),
        P(("dp", "tensor"), None),
        P("dp"),
        P("dp", None, "tensor"),
        P("tensor", "dp"),
        P("dp"),
        P("dp", None, "tensor"),
        P("tensor", "dp"),
    )
    return jax.shard_map(
        on_device, mesh=mesh, in_specs=in_specs, out_specs=out_specs, check_vma=False
    )
```

```python
import jax
import jax.numpy as jnp
from jax import lax
from jax.experimental import pallas as pl
from jax.experimental.pallas import tpu as pltpu
from jax.sharding import PartitionSpec as P

HD = 64
PAIR = 2 * HD
EPS = 1e-05
THETA = 160000.0
NEG = -1e30
LOG2E = 1.4426950408889634
F32 = jnp.float32
BF16 = jnp.bfloat16


def dot(a, b, da, db):
    return lax.dot_general(a, b, (((da,), (db,)), ((), ())), preferred_element_type=F32)


def turn(x, cosine, sine):
    lane = lax.broadcasted_iota(jnp.int32, x.shape, 1)
    other = jnp.where(lane % HD < HD // 2, pltpu.roll(x, PAIR - HD // 2, 1), pltpu.roll(x, HD // 2, 1))
    return x * cosine + other * sine


def norm_parts(values):
    average = jnp.mean(values, axis=-1, keepdims=True)
    centred = values - average
    spread = jnp.mean(centred * centred, axis=-1, keepdims=True)
    scale = lax.rsqrt(spread + EPS)
    return centred * scale, scale


def project(rows, gain_row, weights, cosine, sine, block=256):
    total, width = rows.shape
    wide = weights.shape[0]
    turned = wide // 3 * 2

    def body(rows_ref, gain_ref, w_ref, cos_ref, sin_ref, normed_ref, out_ref):
        xhat, _ = norm_parts(rows_ref[...].astype(F32))
        normed = (xhat * gain_ref[...]).astype(BF16)
        normed_ref[...] = normed
        cos_here, sin_here = cos_ref[...], sin_ref[...]
        for c in range(0, wide, PAIR):
            slab = dot(normed, w_ref[c : c + PAIR, :], 1, 1)
            if c < turned:
                slab = turn(slab, cos_here, sin_here)
            out_ref[:, c : c + PAIR] = slab.astype(BF16)

    row_block = lambda cols: pl.BlockSpec((block, cols), lambda i: (i, 0))
    return pl.pallas_call(
        body,
        grid=(total // block,),
        in_specs=[
            row_block(width),
            pl.BlockSpec((1, width), lambda i: (0, 0)),
            pl.BlockSpec((wide, width), lambda i: (0, 0)),
            row_block(PAIR),
            row_block(PAIR),
        ],
        out_specs=[row_block(width), row_block(wide)],
        out_shape=[
            jax.ShapeDtypeStruct((total, width), BF16),
            jax.ShapeDtypeStruct((total, wide), BF16),
        ],
        name="project",
    )(rows, gain_row, weights, cosine, sine)


def attend(qkv, seg_col, seg_row, block=256):
    total = qkv.shape[0]
    pairs = qkv.shape[1] // 3 // PAIR
    c = HD**-0.5 * LOG2E

    def body(sq_ref, sk_ref, q_ref, k_ref, v_ref, o_ref, lse_ref):
        lane = lax.broadcasted_iota(jnp.int32, (block, PAIR), 1)
        same = sq_ref[...] == sk_ref[...]
        q, k, v = q_ref[...], k_ref[...], v_ref[...]
        out = jnp.zeros((block, PAIR), F32)
        stats = jnp.zeros((block, PAIR), F32)
        for h in range(2):
            own = lane // HD == h
            scores = dot(jnp.where(own, q, jnp.zeros_like(q)), k, 1, 1)
            scores = jnp.where(same, scores, NEG)
            highest = jnp.max(scores, axis=1, keepdims=True)
            weights = jnp.exp2((scores - highest) * c)
            totals = jnp.sum(weights, axis=1, keepdims=True)
            mixed = dot(weights.astype(BF16), v, 1, 0) / totals
            out = jnp.where(own, mixed, out)
            stats = jnp.where(lane == h, highest * c + jnp.log2(totals), stats)
        o_ref[...] = out.astype(BF16)
        lse_ref[...] = stats.T[:8]

    return pl.pallas_call(
        body,
        grid=(pairs, total // block),
        in_specs=[
            pl.BlockSpec((block, 1), lambda p, i: (i, 0)),
            pl.BlockSpec((1, total), lambda p, i: (0, 0)),
            pl.BlockSpec((block, PAIR), lambda p, i: (i, p)),
            pl.BlockSpec((total, PAIR), lambda p, i: (0, pairs + p)),
            pl.BlockSpec((total, PAIR), lambda p, i: (0, 2 * pairs + p)),
        ],
        out_specs=[
            pl.BlockSpec((block, PAIR), lambda p, i: (i, p)),
            pl.BlockSpec((8, block), lambda p, i: (p, i)),
        ],
        out_shape=[
            jax.ShapeDtypeStruct((total, pairs * PAIR), BF16),
            jax.ShapeDtypeStruct((pairs * 8, total), F32),
        ],
        name="attend",
    )(seg_col, seg_row, qkv, qkv, qkv)


def attend_back(qkv, seg_col, seg_row, lse, attended, grad, cosine, sine, block=256, chunk=512):
    total = qkv.shape[0]
    pairs = qkv.shape[1] // 3 // PAIR
    scale = HD**-0.5
    c = scale * LOG2E
    steps = total // block
    chunk = min(chunk, total)

    def body(
        sk_ref, sq_ref, q_ref, k_ref, v_ref, lse_ref, o_ref, do_ref, cosq_ref, sinq_ref, cos_ref,
        sin_ref, dq_ref, dk_ref, dv_ref, kt_ref, dk_acc, dv_acc,
    ):
        i = pl.program_id(1)

        @pl.when(i == 0)
        def _():
            kt_ref[...] = k_ref[...].T
            dk_acc[...] = jnp.zeros_like(dk_acc)
            dv_acc[...] = jnp.zeros_like(dv_acc)

        lane = lax.broadcasted_iota(jnp.int32, (block, PAIR), 1)
        row = lax.broadcasted_iota(jnp.int32, (PAIR, block), 0)
        q, do = q_ref[...], do_ref[...]
        product = do.astype(F32) * o_ref[...].astype(F32)
        product_t = product.T
        heads = []
        for h in range(2):
            own = lane // HD == h
            qh = jnp.where(own, q, jnp.zeros_like(q))
            heads.append((
                qh,
                jnp.where(own, do, jnp.zeros_like(do)),
                (qh.astype(F32) * scale).astype(BF16),
                jnp.sum(product_t[h * HD : (h + 1) * HD], axis=0, keepdims=True),
                lse_ref[h : h + 1, :],
            ))
        sq = sq_ref[...]
        dqt = [jnp.zeros((PAIR, block), F32) for _ in range(2)]
        for at in range(0, total, chunk):
            rows = slice(at, at + chunk)
            k, v = k_ref[rows, :], v_ref[rows, :]
            same = sk_ref[rows, :] == sq
            dk = dv = None
            for h in range(2):
                qh, doh, qs, delta, lse_h = heads[h]
                st = dot(k, qh, 1, 1)
                pt = jnp.exp2(jnp.where(same, st * c - lse_h, NEG))
                dpt = dot(v, doh, 1, 1)
                dst = (pt * (dpt - delta)).astype(BF16)
                dv_h = dot(pt.astype(BF16), doh, 1, 0)
                dk_h = dot(dst, qs, 1, 0)
                dv = dv_h if dv is None else dv + dv_h
                dk = dk_h if dk is None else dk + dk_h
                dqt[h] = dqt[h] + dot(kt_ref[:, rows], dst, 1, 0)
            dk_acc[rows, :] += dk
            dv_acc[rows, :] += dv
        dq = jnp.where(row < HD, dqt[0], dqt[1]).T * scale
        dq_ref[...] = turn(dq, cosq_ref[...], -sinq_ref[...]).astype(BF16)

        @pl.when(i == steps - 1)
        def _():
            dk_ref[...] = turn(dk_acc[...], cos_ref[...], -sin_ref[...]).astype(BF16)
            dv_ref[...] = dv_acc[...].astype(BF16)

    q_block = lambda cols_of: pl.BlockSpec((block, PAIR), lambda p, i: (i, cols_of(p)))
    whole = lambda cols_of: pl.BlockSpec((total, PAIR), lambda p, i: (0, cols_of(p)))
    shape = jax.ShapeDtypeStruct((total, pairs * PAIR), BF16)
    return pl.pallas_call(
        body,
        grid=(pairs, steps),
        in_specs=[
            pl.BlockSpec((total, 1), lambda p, i: (0, 0)),
            pl.BlockSpec((1, block), lambda p, i: (0, i)),
            q_block(lambda p: p),
            whole(lambda p: pairs + p),
            whole(lambda p: 2 * pairs + p),
            pl.BlockSpec((8, block), lambda p, i: (p, i)),
            q_block(lambda p: p),
            q_block(lambda p: p),
            q_block(lambda p: 0),
            q_block(lambda p: 0),
            whole(lambda p: 0),
            whole(lambda p: 0),
        ],
        out_specs=[q_block(lambda p: p), whole(lambda p: p), whole(lambda p: p)],
        out_shape=[shape, shape, shape],
        scratch_shapes=[
            pltpu.VMEM((PAIR, total), BF16),
            pltpu.VMEM((total, PAIR), F32),
            pltpu.VMEM((total, PAIR), F32),
        ],
        name="attend_back",
    )(seg_col, seg_row, qkv, qkv, qkv, lse, attended, grad, cosine, sine, cosine, sine)


def tables(offset):
    lane = jnp.arange(PAIR)
    inverse = THETA ** (-2.0 * (lane % (HD // 2)).astype(F32) / HD)
    angles = offset.astype(F32)[:, None] * inverse[None, :]
    sign = jnp.where(lane % HD < HD // 2, -1.0, 1.0)
    return jnp.cos(angles), jnp.sin(angles) * sign


def gather_line(x, axis):
    n = lax.axis_size(axis)
    here = lax.axis_index(axis)
    to_low = [(i, i - 1) for i in range(1, n)]
    to_high = [(i, i + 1) for i in range(n - 1)]
    from_high, from_low = [x], [x]
    for _ in range(1, n):
        from_high.append(lax.ppermute(from_high[-1], axis, to_low))
        from_low.append(lax.ppermute(from_low[-1], axis, to_high))
    out = jnp.zeros((n,) + x.shape, x.dtype)
    out = lax.dynamic_update_index_in_dim(out, x, here, 0)
    for s in range(1, n):
        piece = jnp.where(here + s < n, from_high[s], from_low[n - s])
        out = lax.dynamic_update_index_in_dim(out, piece, (here + s) % n, 0)
    return out


def scatter_line(parts, axis):
    n = lax.axis_size(axis)
    here = lax.axis_index(axis)

    def take(j):
        return lax.dynamic_index_in_dim(parts, jnp.clip(j, 0, n - 1), 0, keepdims=False)

    low = high = None
    for s in range(1, n):
        send_low = take(here + s - n)
        send_high = take(here + n - s)
        if s > 1:
            send_low = (send_low.astype(F32) + low.astype(F32)).astype(BF16)
            send_high = (send_high.astype(F32) + high.astype(F32)).astype(BF16)
        low = lax.ppermute(send_low, axis, [(i, i - 1) for i in range(n - s, n)])
        high = lax.ppermute(send_high, axis, [(i, i + 1) for i in range(s)])
    return take(here).astype(F32) + low.astype(F32) + high.astype(F32)


def gather_direct(x, axis):
    n = lax.axis_size(axis)
    here = lax.axis_index(axis)
    out = jnp.zeros((n,) + x.shape, x.dtype)
    out = lax.dynamic_update_index_in_dim(out, x, here, 0)
    for s in range(1, n):
        piece = lax.ppermute(x, axis, [(i, (i + s) % n) for i in range(n)])
        out = lax.dynamic_update_index_in_dim(out, piece, (here - s) % n, 0)
    return out


def scatter_direct(parts, axis):
    return jnp.sum(lax.all_to_all(parts, axis, 0, 0, tiled=True).astype(F32), axis=0)


def places(order_row, length_row):
    bounds = jnp.cumsum(length_row)
    passed = (order_row[:, None] >= bounds[None, :]).astype(jnp.int32)
    segment = jnp.sum(passed, axis=1)
    offset = order_row - jnp.sum(passed * length_row[None, :], axis=1)
    return (segment, offset)


def norm_back(grad_n, xhat, scale, gain_row):
    e = grad_n * gain_row
    return (
        e
        - jnp.mean(e, axis=-1, keepdims=True)
        - xhat * jnp.mean(e * xhat, axis=-1, keepdims=True)
    ) * scale


def on_device(
    tokens, lengths, order, gain_attn, w_qkv, w_attn_out, gain_mlp, w_in, w_mlp_out, grad_out
):
    tensor_size = lax.axis_size("tensor")
    local_rows, width = tokens.shape
    group_rows = local_rows * tensor_size
    piece = w_qkv.shape[0]
    heads_wide = w_qkv.shape[2]
    units = w_in.shape[2]
    segment, offset = places(order[0], lengths[0])
    cosine, sine = tables(offset)
    seg_col, seg_row = segment[:, None], segment[None, :]

    gains_low = jnp.zeros((16, piece), BF16).at[0].set(gain_attn).at[1].set(gain_mlp)
    qkv_rows = jnp.concatenate(
        [w_qkv.transpose(1, 2, 0).reshape(3 * heads_wide, piece), gains_low], axis=0
    )
    qkv_rows = lax.all_gather(qkv_rows, "dp", axis=1, tiled=True)
    qkv_t = qkv_rows[: 3 * heads_wide]
    gain_one = qkv_rows[3 * heads_wide : 3 * heads_wide + 1].astype(F32)
    gain_two = qkv_rows[3 * heads_wide + 1 : 3 * heads_wide + 2].astype(F32)

    w_in_t = w_in.transpose(1, 2, 0)

    def over_dp(part):
        return lax.all_gather(part.reshape(-1, piece), "dp", axis=1, tiled=True)

    first = gather_direct(jnp.concatenate([w_attn_out, w_in_t[0]], axis=0), "tensor")
    rows_all = gather_line(tokens, "tensor").reshape(group_rows, width)
    rest, _ = lax.optimization_barrier(
        (jnp.concatenate([w_in_t[1], w_mlp_out], axis=0), rows_all[:8, :128])
    )
    second = gather_direct(rest, "tensor")
    w_ao = over_dp(first[:, :heads_wide])
    w_gate = over_dp(first[:, heads_wide:])
    w_up = over_dp(second[:, :units])
    w_down = over_dp(second[:, units:])

    rows_one, qkv = project(rows_all, gain_one, qkv_t, cosine, sine)
    mixed, lse = attend(qkv, seg_col, seg_row)
    attended = lax.all_to_all(mixed, "tensor", split_axis=0, concat_axis=1, tiled=True)

    inputs = tokens.astype(F32)
    middle = inputs + dot(attended, w_ao, 1, 0)
    xhat_two, scale_two = norm_parts(middle)
    rows_two = (xhat_two * gain_two).astype(BF16)
    gate = dot(rows_two, w_gate, 1, 1)
    up = dot(rows_two, w_up, 1, 1)
    grad_act = dot(grad_out, w_down, 1, 1)
    cdf = 0.5 * (1.0 + lax.erf(gate * (0.5**0.5)))
    density = jnp.exp(-0.5 * gate * gate) * 0.3989422804014327
    bent = gate * cdf
    activated = (bent * up).astype(BF16)
    grad_gate = (grad_act * up * (cdf + gate * density)).astype(BF16)
    grad_up = (grad_act * bent).astype(BF16)
    result = (middle + dot(activated, w_down, 1, 0)).astype(BF16)
    grad_normed_two = dot(grad_gate, w_gate, 1, 0) + dot(grad_up, w_up, 1, 0)
    grad_middle = grad_out.astype(F32) + norm_back(grad_normed_two, xhat_two, scale_two, gain_two)
    gain_two_part = jnp.sum(grad_normed_two * xhat_two, axis=0)
    grad_branch = grad_middle.astype(BF16)
    grad_attended = dot(grad_branch, w_ao, 1, 1).astype(BF16)
    grad_mixed = lax.all_to_all(
        grad_attended, "tensor", split_axis=1, concat_axis=0, tiled=True
    )

    def over_rows(a, b):
        return lax.psum_scatter(
            dot(a, b, 0, 0).astype(BF16), "dp", scatter_dimension=0, tiled=True
        )

    sum_down = over_rows(grad_out, activated)
    sum_gate = over_rows(rows_two, grad_gate)
    sum_up = over_rows(rows_two, grad_up)
    sum_ao = over_rows(grad_branch, attended)

    grad_q, grad_k, grad_v = attend_back(
        qkv, seg_col, seg_row, lse, mixed, grad_mixed, cosine, sine
    )
    grad_projected = jnp.concatenate([grad_q, grad_k, grad_v], axis=1)
    part_one = dot(grad_projected, qkv_t, 1, 0)
    xhat_all, _ = norm_parts(rows_all.astype(F32))
    gain_one_part = jnp.sum(part_one * xhat_all, axis=0)
    part_one = part_one.astype(BF16).reshape(tensor_size, local_rows, width)
    grad_normed_one = scatter_line(part_one, "tensor")
    grad_qkv_rows = dot(rows_one, grad_projected, 0, 0).astype(BF16)
    gain_cols = jnp.stack([gain_one_part, gain_two_part], axis=1).astype(BF16)
    gain_cols = jnp.pad(gain_cols, ((0, 0), (0, 126)))
    sum_qkv = lax.psum_scatter(
        jnp.concatenate([grad_qkv_rows, gain_cols], axis=1), "dp", scatter_dimension=0, tiled=True
    )

    xhat_one, scale_one = norm_parts(inputs)
    grad_tokens = grad_middle + norm_back(grad_normed_one, xhat_one, scale_one, gain_one)

    def apart(part):
        return part.reshape(piece, tensor_size, -1).transpose(1, 0, 2)

    grad_down = scatter_direct(apart(sum_down), "tensor").T
    grad_gate_w = scatter_direct(apart(sum_gate), "tensor")
    grad_up_w = scatter_direct(apart(sum_up), "tensor")
    gain_copies = jnp.broadcast_to(
        sum_qkv[None, :, 3 * heads_wide :], (tensor_size, piece, 128)
    )
    last = scatter_direct(jnp.concatenate([apart(sum_ao), gain_copies], axis=2), "tensor")
    grad_ao = last[:, :heads_wide].T
    gain_sums = last[:, heads_wide : heads_wide + 2].T
    grad_in = jnp.stack([grad_gate_w, grad_up_w], axis=1)
    grad_qkv = sum_qkv[:, : 3 * heads_wide].astype(F32).reshape(piece, 3, heads_wide)
    return (
        result,
        grad_tokens.astype(BF16),
        gain_sums[0],
        grad_qkv,
        grad_ao,
        gain_sums[1],
        grad_in,
        grad_down,
    )


def solution(mesh):
    in_specs = (
        P(("dp", "tensor"), None),
        P("dp", None),
        P("dp", None),
        P("dp"),
        P("dp", None, "tensor"),
        P("tensor", "dp"),
        P("dp"),
        P("dp", None, "tensor"),
        P("tensor", "dp"),
        P(("dp", "tensor"), None),
    )
    out_specs = (
        P(("dp", "tensor"), None),
        P(("dp", "tensor"), None),
        P("dp"),
        P("dp", None, "tensor"),
        P("tensor", "dp"),
        P("dp"),
        P("dp", None, "tensor"),
        P("tensor", "dp"),
    )
    return jax.shard_map(
        on_device, mesh=mesh, in_specs=in_specs, out_specs=out_specs, check_vma=False
    )
```
